32 devices in a mesh: dp: 8 (over y, x, core), ctx: 4 (over z).
Axes of the slice: x: 2, y: 2, z: 4, core: 2. Of those that a mesh axis runs over, the one named last changes fastest.
Arguments:
- tokens: bfloat16 [24, 384, 1024], P('dp', 'ctx'), may hold values from -6 to 6
- block_counts: int32 [24, 4], P('dp'), may hold values from 1 to 96, as said below
- qkv_weight: bfloat16 [1024, 3072], P(('dp', 'ctx')), may hold values from -2 to 2
- proj_weight: bfloat16 [1024, 1024], P(('dp', 'ctx')), may hold values from -4 to 4
- expand_weight: bfloat16 [1024, 4096], P(('dp', 'ctx')), may hold values from -0.1875 to 0.1875
- reduce_weight: bfloat16 [4096, 1024], P(('dp', 'ctx')), may hold values from -0.09375 to 0.09375
- vectors: bfloat16 [10, 1024], P(None, ('dp', 'ctx')), may hold values from -2.5 to 2.5
- expand_bias: bfloat16 [4096], P(('dp', 'ctx')), may hold values from -3 to 3
- cotangent: bfloat16 [24, 384, 1024], P('dp', 'ctx'), may hold values from -6 to 6
Outputs:
- output: bfloat16 [24, 384, 1024], P('dp', 'ctx')
- input_grad: bfloat16 [24, 384, 1024], P('dp', 'ctx')
- qkv_grad: float32 [1024, 3072], P(('dp', 'ctx'))
- proj_grad: float32 [1024, 1024], P(('dp', 'ctx'))
- expand_grad: float32 [1024, 4096], P(('dp', 'ctx'))
- reduce_grad: float32 [4096, 1024], P(('dp', 'ctx'))
- vector_grad: float32 [10, 1024], P(None, ('dp', 'ctx'))
- bias_grad: float32 [4096], P(('dp', 'ctx'))
The draws below stay inside these ranges and needn't reach their ends.
Inputs may be any that keep to these rules, and one draw needn't show every extreme that they name: `block_counts`: in every image the blocks on the first 3 devices of the context group are full with 96 tokens; only the last block is ragged.
All inputs are finite; a program needn't handle non-finite values.
Results may differ from the reference program's by a relative error of at most 0.014.
Values may be sent and summed in bfloat16 or wider, within the bound.
No kernel may reach another device: no remote copies, remote signals or barrier semaphores. Data moves between devices by JAX's collectives and lax.ppermute only.
A program may use at most 256 MiB of HBM per device.

```python
import math
import jax
import jax.numpy as jnp
from jax import lax

D = 1024
FF = 4096
HD = 64
H = 16
TB = 96
SLOTS = 384
IMAGES = 24


def draw_block_counts(key, part):
    last_block = jax.random.randint(key, (IMAGES, 1), 1, TB + 1, dtype=jnp.int32)
    full_blocks = jnp.full((IMAGES, SLOTS // TB - 1), TB, jnp.int32)
    return jnp.concatenate([full_blocks, last_block], axis=1)


def draw_qkv_weight(key, part):
    base_key = jax.random.fold_in(key, 11)
    result = jnp.clip(jax.random.normal(base_key, (D, 3 * D), jnp.float32), -6.0, 6.0) / math.sqrt(D)
    return result.astype(jnp.bfloat16)


def draw_vectors(key, part):
    gain_key = jax.random.fold_in(key, 21)
    shift_key = jax.random.fold_in(key, 22)
    layer_key = jax.random.fold_in(key, 23)
    gains = 1.0 + jnp.clip(0.15 * jax.random.normal(gain_key, (2, D), jnp.float32), -0.6, 0.6)
    shifts = jnp.clip(0.4 * jax.random.normal(shift_key, (6, D), jnp.float32), -2.4, 2.4)
    layer_scales = jnp.exp(jax.random.uniform(layer_key, (2, D), jnp.float32, math.log(0.3), math.log(1.5)))
    result = jnp.stack([gains[0], shifts[0], shifts[1], shifts[2], shifts[3], layer_scales[0], gains[1], shifts[4], shifts[5], layer_scales[1]])
    return result.astype(jnp.bfloat16)


def shard_levels(stream_key, dims, cuts, least, high):
    level, own = 1.0, jax.random.fold_in(stream_key, 6)
    for axis_at, shards_of in cuts:
        steps = jnp.exp(jax.random.uniform(jax.random.fold_in(own, axis_at), (shards_of,), jnp.float32, least / len(cuts), high / len(cuts)))
        level = level * jnp.repeat(steps, dims[axis_at] // shards_of).reshape([-1 if axis == axis_at else 1 for axis in range(len(dims))])
    return level


def centred(rng, dims, scale, reach, split=(), kind=jnp.bfloat16):
    level = shard_levels(rng, dims, split, -0.22, 0.18) if split else 1.0
    values = jax.random.normal(rng, dims, jnp.float32) * scale * level
    return jnp.minimum(jnp.maximum(values, -reach), reach).astype(kind)


def setup_inputs(seed: int = 0) -> dict:
    splits = jax.random.split(jax.random.key(seed), 10)
    return {
        "tokens": centred(splits[0], (IMAGES, SLOTS, D), 1.0, 6.0, ((0, 8), (1, 4))),
        "block_counts": draw_block_counts(jax.random.fold_in(splits[9], 71), 0),
        "qkv_weight": draw_qkv_weight(jax.random.fold_in(splits[9], 71), 0),
        "proj_weight": centred(splits[3], (D, D), (max(D // 512, 1)) ** -0.5, 4.0, ((0, 32),)),
        "expand_weight": centred(splits[4], (D, FF), D ** -0.5, 0.1875, ((0, 32),)),
        "reduce_weight": centred(splits[5], (FF, D), FF ** -0.5, 0.09375, ((0, 32),)),
        "vectors": draw_vectors(jax.random.fold_in(splits[9], 71), 0),
        "expand_bias": centred(splits[7], (FF,), 0.5, 3.0, ((0, 32),)),
        "cotangent": centred(splits[8], (IMAGES, SLOTS, D), 1.0, 6.0, ((0, 8), (1, 4))),
    }


EPSILON = 1e-06
SQRT_HALF = 0.7071067811865476
INV_SQRT_TAU = 0.3989422804014327

def layer_norm(values, gain_row, shift_row):
    center = values - lax.optimization_barrier(jnp.mean(values, axis=-1, keepdims=True))
    inv_std = lax.rsqrt(lax.optimization_barrier(jnp.mean(center * center, axis=-1, keepdims=True)) + EPSILON)
    normed = center * inv_std
    return (normed * gain_row + shift_row, normed, inv_std)

def norm_back(grad_out, normed, inv_std, gain_row):
    scaled = grad_out * gain_row
    return inv_std * (scaled - lax.optimization_barrier(jnp.mean(scaled, axis=-1, keepdims=True)) - normed * lax.optimization_barrier(jnp.mean(scaled * normed, axis=-1, keepdims=True)))

def gelu_value(pre_act):
    return 0.5 * pre_act * (1.0 + jax.scipy.special.erf(pre_act * SQRT_HALF))

def gelu_slope(pre_act):
    return 0.5 * (1.0 + jax.scipy.special.erf(pre_act * SQRT_HALF)) + pre_act * jnp.exp(-0.5 * pre_act * pre_act) * INV_SQRT_TAU

def split_heads(tensor):
    return tensor.reshape(SLOTS, H, HD).transpose(1, 0, 2)

def merge_heads(tensor):
    return tensor.transpose(1, 0, 2).reshape(SLOTS, D)

def head_scores(query_head, key_head, key_valid):
    scores = jnp.dot(query_head, key_head.T, preferred_element_type=jnp.float32) * 0.125
    return jnp.where(key_valid[None, :], scores, -jnp.inf)

def reference(tokens, block_counts, qkv_weight, proj_weight, expand_weight, reduce_weight, vectors, expand_bias, cotangent):
    params = vectors.astype(jnp.float32)
    bias_row = expand_bias.astype(jnp.float32)

    def image_step(running, pieces):
        tokens_img, counts_img, cot_img = pieces
        slot_iota = jnp.arange(TB, dtype=jnp.int32)
        key_valid = (slot_iota[None, :] < counts_img[:, None]).reshape(SLOTS)
        row_valid = key_valid.astype(jnp.float32)[:, None]
        inputs = tokens_img.astype(jnp.float32)
        hidden_one, normed_one, inv_one = layer_norm(inputs, params[0], params[1])
        hidden_one = hidden_one.astype(jnp.bfloat16)
        mixed_rows = jnp.dot(hidden_one, qkv_weight, preferred_element_type=jnp.float32)
        queries = (mixed_rows[:, :D] + params[2]).astype(jnp.bfloat16)
        key_rows = mixed_rows[:, D:2 * D].astype(jnp.bfloat16)
        value_rows = (mixed_rows[:, 2 * D:] + params[3]).astype(jnp.bfloat16)

        def head_forward(head_parts):
            query_head, key_head, value_head = head_parts
            scores = head_scores(query_head, key_head, key_valid)
            row_peak = lax.optimization_barrier(jnp.max(scores, axis=-1, keepdims=True))
            log_total = row_peak + jnp.log(lax.optimization_barrier(jnp.sum(jnp.exp(scores - row_peak), axis=-1, keepdims=True)))
            prob_bf = jnp.exp(scores - log_total).astype(jnp.bfloat16)
            attended_head = jnp.dot(prob_bf, value_head, preferred_element_type=jnp.float32).astype(jnp.bfloat16)
            return (attended_head, log_total)
        attended_heads, log_totals = lax.map(head_forward, (split_heads(queries), split_heads(key_rows), split_heads(value_rows)))
        attended = merge_heads(attended_heads)
        branch_one = jnp.dot(attended, proj_weight, preferred_element_type=jnp.float32) + params[4]
        middle = inputs + params[5] * branch_one
        hidden_two, normed_two, inv_two = layer_norm(middle, params[6], params[7])
        hidden_two = hidden_two.astype(jnp.bfloat16)
        pre_act = jnp.dot(hidden_two, expand_weight, preferred_element_type=jnp.float32) + bias_row
        activated = gelu_value(pre_act).astype(jnp.bfloat16)
        branch_two = jnp.dot(activated, reduce_weight, preferred_element_type=jnp.float32) + params[8]
        output = (row_valid * (middle + params[9] * branch_two)).astype(jnp.bfloat16)
        grad_y = cot_img.astype(jnp.float32) * row_valid
        scaled_two = params[9] * grad_y
        scaled_two_bf = scaled_two.astype(jnp.bfloat16)
        grad_pre = jnp.dot(scaled_two_bf, reduce_weight.T, preferred_element_type=jnp.float32) * gelu_slope(pre_act)
        grad_pre_bf = grad_pre.astype(jnp.bfloat16)
        grad_hidden_two = jnp.dot(grad_pre_bf, expand_weight.T, preferred_element_type=jnp.float32)
        grad_middle = grad_y + norm_back(grad_hidden_two, normed_two, inv_two, params[6])
        scaled_one = params[5] * grad_middle
        scaled_one_bf = scaled_one.astype(jnp.bfloat16)
        grad_attended = jnp.dot(scaled_one_bf, proj_weight.T, preferred_element_type=jnp.float32).astype(jnp.bfloat16)

        def head_backward(head_parts):
            query_head, key_head, value_head, out_head, grad_head, log_total = head_parts
            scores = head_scores(query_head, key_head, key_valid)
            prob_f = jnp.exp(scores - log_total)
            prob_bf = prob_f.astype(jnp.bfloat16)
            delta = lax.optimization_barrier(jnp.sum(grad_head.astype(jnp.float32) * out_head.astype(jnp.float32), axis=-1, keepdims=True))
            grad_prob = jnp.dot(grad_head, value_head.T, preferred_element_type=jnp.float32)
            grad_scores = (prob_f * (grad_prob - delta) * 0.125).astype(jnp.bfloat16)
            grad_query = jnp.dot(grad_scores, key_head, preferred_element_type=jnp.float32)
            grad_key = jnp.dot(grad_scores.T, query_head, preferred_element_type=jnp.float32)
            grad_value = jnp.dot(prob_bf.T, grad_head, preferred_element_type=jnp.float32)
            return (grad_query, grad_key, grad_value)
        head_grads = lax.map(head_backward, (split_heads(queries), split_heads(key_rows), split_heads(value_rows), attended_heads, split_heads(grad_attended), log_totals))
        grad_queries = merge_heads(head_grads[0])
        grad_keys = merge_heads(head_grads[1])
        grad_values = merge_heads(head_grads[2])
        grad_mixed = jnp.concatenate([grad_queries, grad_keys, grad_values], axis=-1).astype(jnp.bfloat16)
        grad_hidden_one = jnp.dot(grad_mixed, qkv_weight.T, preferred_element_type=jnp.float32)
        input_grad = (grad_middle + norm_back(grad_hidden_one, normed_one, inv_one, params[0])).astype(jnp.bfloat16)
        vector_terms = jnp.stack([lax.optimization_barrier(jnp.sum(grad_hidden_one * normed_one, axis=0)), lax.optimization_barrier(jnp.sum(grad_hidden_one, axis=0)), lax.optimization_barrier(jnp.sum(grad_queries, axis=0)), lax.optimization_barrier(jnp.sum(grad_values, axis=0)), lax.optimization_barrier(jnp.sum(scaled_one, axis=0)), lax.optimization_barrier(jnp.sum(grad_middle * branch_one, axis=0)), lax.optimization_barrier(jnp.sum(grad_hidden_two * normed_two, axis=0)), lax.optimization_barrier(jnp.sum(grad_hidden_two, axis=0)), lax.optimization_barrier(jnp.sum(scaled_two, axis=0)), lax.optimization_barrier(jnp.sum(grad_y * branch_two, axis=0))])
        updated = (running[0] + jnp.dot(hidden_one.T, grad_mixed, preferred_element_type=jnp.float32), running[1] + jnp.dot(attended.T, scaled_one_bf, preferred_element_type=jnp.float32), running[2] + jnp.dot(hidden_two.T, grad_pre_bf, preferred_element_type=jnp.float32), running[3] + jnp.dot(activated.T, scaled_two_bf, preferred_element_type=jnp.float32), running[4] + vector_terms, running[5] + lax.optimization_barrier(jnp.sum(grad_pre, axis=0)))
        return (updated, (output, input_grad))
    start = (jnp.zeros((D, 3 * D), jnp.float32), jnp.zeros((D, D), jnp.float32), jnp.zeros((D, FF), jnp.float32), jnp.zeros((FF, D), jnp.float32), jnp.zeros((10, D), jnp.float32), jnp.zeros((FF,), jnp.float32))
    totals, stacked = lax.scan(image_step, start, (tokens, block_counts, cotangent))
    return (stacked[0], stacked[1], totals[0], totals[1], totals[2], totals[3], totals[4], totals[5])
```

```python
import functools

import jax
import jax.numpy as jnp
from jax import lax
from jax.experimental import pallas as pl
from jax.experimental.pallas import tpu as pltpu
from jax.sharding import PartitionSpec as P

HD = 64
PAIR = 2 * HD
LANES = 128
EPSILON = 1e-06
SQRT_HALF = 0.7071067811865476
INV_SQRT_TAU = 0.3989422804014327
BF = jnp.bfloat16
F32 = jnp.float32
ANY = pl.BlockSpec(memory_space=pl.ANY)
SCALE = 0.125


def bits_of(size):
    return size.bit_length() - 1


def swap(value, axis, distance):
    count = lax.axis_size(axis)
    return lax.ppermute(value, axis, [(i, i ^ distance) for i in range(count)])


def insert_bit(other, at, bit):
    return ((other >> at) << (at + 1)) | (bit << at) | (other & ((1 << at) - 1))


def remove_bit(index, at):
    return ((index >> (at + 1)) << at) | (index & ((1 << at) - 1))


def bit_at(index, at):
    return (index >> at) & 1


def join(mine, other, flag, axis):
    low = jnp.where(flag, other, mine)
    high = jnp.where(flag, mine, other)
    return jnp.stack([low, high], axis=axis)


def dot(a, b):
    return lax.dot_general(a, b, (((1,), (0,)), ((), ())), preferred_element_type=F32)


def dot_tb(a, b):
    return lax.dot_general(a, b, (((1,), (1,)), ((), ())), preferred_element_type=F32)


def dot_ta(a, b):
    return lax.dot_general(a, b, (((0,), (0,)), ((), ())), preferred_element_type=F32)


def normalize(values):
    center = values - jnp.mean(values, axis=-1, keepdims=True)
    inv_std = lax.rsqrt(jnp.mean(center * center, axis=-1, keepdims=True) + EPSILON)
    return center * inv_std, inv_std


def norm_back(grad_out, normed, inv_std, gain_row):
    scaled = grad_out * gain_row
    return inv_std * (
        scaled
        - jnp.mean(scaled, axis=-1, keepdims=True)
        - normed * jnp.mean(scaled * normed, axis=-1, keepdims=True)
    )


def col_sum(value):
    return jnp.sum(value, axis=0, keepdims=True)


def call(kernel, name, out_shapes, args, in_specs, out_specs, grid=(1,), scalars=(), scratch=(), flops=0, limit=40):
    nbytes = sum(a.size * a.dtype.itemsize for a in args)
    nbytes += sum(o.size * o.dtype.itemsize for o in out_shapes)
    return pl.pallas_call(
        kernel,
        name=name,
        out_shape=tuple(out_shapes),
        grid_spec=pltpu.PrefetchScalarGridSpec(
            num_scalar_prefetch=len(scalars),
            grid=grid,
            in_specs=list(in_specs),
            out_specs=tuple(out_specs),
            scratch_shapes=list(scratch),
        ),
        compiler_params=pltpu.CompilerParams(
            dimension_semantics=("arbitrary",) * len(grid), vmem_limit_bytes=limit << 20
        ),
        cost_estimate=pl.CostEstimate(flops=int(flops), bytes_accessed=int(nbytes), transcendentals=0),
    )(*scalars, *args)


def whole(shape):
    zeros = (0,) * len(shape)
    return pl.BlockSpec(tuple(shape), lambda *_: zeros)


def start_all(copies, sems, first=0):
    handles = []
    for n, (src, dst) in enumerate(copies):
        handle = pltpu.make_async_copy(src, dst, sems.at[first + n])
        handle.start()
        handles.append(handle)
    return handles


def core_copies(own, other, dst, core):
    n_chips, rows, _ = own.shape
    copies = []
    for chip in range(n_chips):
        for ref, side in ((own, core), (other, 1 - core)):
            at = pl.multiple_of((chip * 2 + side) * rows, rows)
            copies.append((ref.at[chip], dst.at[pl.ds(at, rows), :]))
    return copies


def chip_copies(own, other, dst, chip, last, rows, first_row, columns):
    copies = []
    for rest in range(own.shape[0]):
        for ref, flip in ((own, 0), (other, 1)):
            at = insert_bit(rest, last, bit_at(chip, last) ^ flip)
            at = pl.multiple_of(at * rows, rows)
            copies.append(
                (ref.at[rest, pl.ds(first_row, rows), :], dst.at[pl.ds(at, rows), pl.ds(columns, ref.shape[-1])])
            )
    return copies


def key_mask(counts, image, n_blocks, block_len):
    slot = lax.broadcasted_iota(jnp.int32, (1, n_blocks * block_len), 1)
    valid = slot < 0
    for block in range(n_blocks):
        here = slot - block * block_len
        valid = valid | ((here >= 0) & (here < counts[image, block]))
    return valid


def head_halves():
    lane = lax.broadcasted_iota(jnp.int32, (1, PAIR), 1)
    low = lane < HD
    masks = (jnp.where(low, 1.0, 0.0).astype(BF), jnp.where(low, 0.0, 1.0).astype(BF))
    return low, masks


def stacked_rows(refs):
    rows = []
    for ref in refs:
        value = ref[...]
        rows.append(value.reshape(-1, value.shape[-1]))
    return jnp.concatenate(rows, axis=0)


def attend_kernel(sizes, ids, counts, *refs):
    n_pieces, n_blocks, block_len, width, group = sizes
    pieces, refs = refs[:n_pieces], refs[n_pieces:]
    w_own, w_other, refs = refs[0], refs[1], refs[2:]
    params_ref, hidden_ref, mixed_ref, total_ref = refs[:4]
    attended_refs, (weight, sems) = refs[4 : 4 + n_blocks], refs[4 + n_blocks :]
    core, z = ids[1], ids[2]
    image = pl.program_id(0)

    @pl.when(image == 0)
    def _():
        for handle in start_all(core_copies(w_own, w_other, weight, core), sems):
            handle.wait()
        tail = weight[:, 3 * group :].astype(F32)
        params_ref[...] = tail.T[:16]

    inputs = stacked_rows(pieces).astype(F32)
    normed, _ = normalize(inputs)
    hidden = (normed * params_ref[0:1, :] + params_ref[1:2, :]).astype(BF)
    hidden_ref[0] = hidden
    mixed = dot(hidden, weight[:, : 3 * group])
    own = pl.ds(pl.multiple_of(z * group, group), group)
    queries = (mixed[:, :group] + params_ref[2:3, own]).astype(BF)
    keys = mixed[:, group : 2 * group].astype(BF)
    values = (mixed[:, 2 * group :] + params_ref[3:4, own]).astype(BF)
    mixed_ref[0, :, :group] = queries
    mixed_ref[0, :, group : 2 * group] = keys
    mixed_ref[0, :, 2 * group :] = values
    valid = key_mask(counts, image, n_blocks, block_len)
    low, masks = head_halves()
    lane = lax.broadcasted_iota(jnp.int32, (1, LANES), 1)
    totals = jnp.zeros((n_blocks * block_len, LANES), F32)
    for pair in range(group // PAIR):
        cols = slice(pair * PAIR, (pair + 1) * PAIR)
        outs = []
        for side in range(2):
            scores = dot_tb(queries[:, cols] * masks[side], keys[:, cols]) * SCALE
            scores = jnp.where(valid, scores, -jnp.inf)
            peak = jnp.max(scores, axis=-1, keepdims=True)
            total = peak + jnp.log(jnp.sum(jnp.exp(scores - peak), axis=-1, keepdims=True))
            probs = jnp.exp(scores - total).astype(BF)
            outs.append(dot(probs, values[:, cols]))
            totals = jnp.where(lane == 2 * pair + side, total, totals)
        attended = jnp.where(low, outs[0], outs[1]).astype(BF)
        for block, ref in enumerate(attended_refs):
            ref[0, :, cols] = attended[block * block_len : (block + 1) * block_len]
    total_ref[0] = totals


def piece_specs(pieces, block_len, width):
    specs = []
    for piece in pieces:
        lead = piece.shape[:-3]
        specs.append(
            pl.BlockSpec(
                lead + (1, block_len, width), functools.partial(lambda n, i, *_: (0,) * n + (i, 0, 0), len(lead))
            )
        )
    return specs


def per_image(shape):
    return pl.BlockSpec((1,) + tuple(shape), lambda i, *_: (i,) + (0,) * len(shape))


def attend(ids, counts, pieces, w_own, w_other, n_blocks, group):
    n_images, block_len, width = pieces[0].shape
    slots = n_blocks * block_len
    sizes = (len(pieces), n_blocks, block_len, width, group)
    outs = [
        jax.ShapeDtypeStruct((16, width), F32),
        jax.ShapeDtypeStruct((n_images, slots, width), BF),
        jax.ShapeDtypeStruct((n_images, slots, 3 * group), BF),
        jax.ShapeDtypeStruct((n_images, slots, LANES), F32),
    ] + [jax.ShapeDtypeStruct((n_images, block_len, group), BF)] * n_blocks
    out_specs = [whole((16, width)), per_image((slots, width)), per_image((slots, 3 * group)), per_image((slots, LANES))]
    out_specs += [per_image((block_len, group))] * n_blocks
    return call(
        functools.partial(attend_kernel, sizes),
        "attend",
        outs,
        (*pieces, w_own, w_other),
        piece_specs(pieces, block_len, width) + [ANY, ANY],
        out_specs,
        grid=(n_images,),
        scalars=(ids, counts),
        scratch=[pltpu.VMEM((width, w_own.shape[-1]), BF), pltpu.SemaphoreType.DMA((2 * w_own.shape[0],))],
        flops=n_images * 2 * slots * group * (3 * width + 4 * slots),
    )


def project_kernel(layout, ids, *refs):
    n_att, chunk_rows, group = layout
    att, refs = refs[:n_att], refs[n_att:]
    tokens, w_own, w_other, params, refs = refs[0], refs[1], refs[2], refs[3], refs[4:]
    attended_ref, branch_ref, middle_ref, hidden_ref, weight, att_scr, sems = refs
    core, z = ids[1], ids[2]
    handles = start_all(core_copies(w_own, w_other, weight, core), sems)
    copies = []
    for n, (rel, first, rows) in enumerate(chunk_rows):
        at = pl.multiple_of((z ^ rel) * group, group)
        copies.append((att[n], att_scr.at[pl.ds(first, rows), pl.ds(at, group)]))
    handles += start_all(copies, sems, len(handles))
    for handle in handles:
        handle.wait()
    attended = att_scr[...]
    attended_ref[...] = attended
    branch = dot(attended, weight[...]) + params[4:5, :]
    branch_ref[...] = branch
    middle = tokens[...].astype(F32) + params[5:6, :] * branch
    middle_ref[...] = middle
    normed, _ = normalize(middle)
    hidden_ref[...] = (normed * params[6:7, :] + params[7:8, :]).astype(BF)


def project(ids, att, chunk_rows, group, tokens, w_own, w_other, params):
    rows, width = tokens.shape
    n_sems = 2 * w_own.shape[0] + len(att)
    return call(
        functools.partial(project_kernel, (len(att), chunk_rows, group)),
        "project",
        [
            jax.ShapeDtypeStruct((rows, width), BF),
            jax.ShapeDtypeStruct((rows, width), F32),
            jax.ShapeDtypeStruct((rows, width), F32),
            jax.ShapeDtypeStruct((rows, width), BF),
        ],
        (*att, tokens, w_own, w_other, params),
        [ANY] * len(att) + [whole((rows, width)), ANY, ANY, whole(params.shape)],
        [whole((rows, width))] * 4,
        scalars=(ids,),
        scratch=[
            pltpu.VMEM((width, width), BF),
            pltpu.VMEM((rows, width), BF),
            pltpu.SemaphoreType.DMA((n_sems,)),
        ],
        flops=2 * rows * width * width,
    )


def expand_copies(refs, dst, chip, rows, halves):
    copies = []
    for n, (own, other, last) in enumerate(refs):
        copies.append(chip_copies(own, other, dst, chip, last, rows, 0, n * halves))
    return copies


def expand_kernel(layout, ids, hid_own, hid_other, bias, a_own, a_other, b_own, b_other, act_ref, slope_ref, weight, sems):
    rows, half, chunk, lasts = layout
    chip = ids[0]
    parts = expand_copies(((a_own, a_other, lasts[0]), (b_own, b_other, lasts[1])), weight, chip, rows, half)
    step = pl.program_id(0)

    def handles(start):
        out, first = [], 0
        for part in parts:
            made = [pltpu.make_async_copy(s, d, sems.at[first + n]) for n, (s, d) in enumerate(part)]
            first += len(part)
            out.append(made)
        return out

    made = handles(True)

    @pl.when(step == 0)
    def _():
        for part in made:
            for handle in part:
                handle.start()
        for handle in made[0]:
            handle.wait()

    @pl.when(step == half // chunk)
    def _():
        for handle in made[1]:
            handle.wait()

    cols = pl.ds(pl.multiple_of(step * chunk, chunk), chunk)
    block = weight[:, cols]
    n_rows = hid_own.shape[0]
    for side, hid in enumerate((hid_own, hid_other)):
        pre = dot(hid[...], block) + bias[...]
        gate = 0.5 * (1.0 + lax.erf(pre * SQRT_HALF))
        at = slice(side * n_rows, (side + 1) * n_rows)
        act_ref[at, :] = (pre * gate).astype(BF)
        slope_ref[at, :] = gate + pre * jnp.exp(-0.5 * pre * pre) * INV_SQRT_TAU


def expand(ids, hid_own, hid_other, bias, weights, lasts, rows, chunk):
    n_rows, width = hid_own.shape
    hidden = bias.shape[-1]
    half = hidden // 2
    n_sems = 4 * weights[0].shape[0]
    return call(
        functools.partial(expand_kernel, (rows, half, chunk, lasts)),
        "expand",
        [jax.ShapeDtypeStruct((2 * n_rows, hidden), BF), jax.ShapeDtypeStruct((2 * n_rows, hidden), F32)],
        (hid_own, hid_other, bias, *weights),
        [whole((n_rows, width))] * 2 + [pl.BlockSpec((1, chunk), lambda i, *_: (0, i))] + [ANY] * 4,
        [pl.BlockSpec((2 * n_rows, chunk), lambda i, *_: (0, i))] * 2,
        grid=(hidden // chunk,),
        scalars=(ids,),
        scratch=[pltpu.VMEM((width, hidden), BF), pltpu.SemaphoreType.DMA((n_sems,))],
        flops=4 * n_rows * width * hidden,
    )


def reduce_kernel(
    layout, ids, s_own, s_other, act, slope, ea_own, ea_other, eb_own, eb_other, ra_own, ra_other, rb_own, rb_other,
    grad_pre_ref, bias_ref, grad_own_ref, grad_send_ref, branch_own_ref, branch_send_ref,
    w_expand, w_reduce, acc_grad, acc_branch, sems,
):
    e_rows, e_half, r_rows, r_half, lasts, chunk = layout
    chip = ids[0]
    step = pl.program_id(0)
    parts = expand_copies(((ra_own, ra_other, lasts[0]), (rb_own, rb_other, lasts[1])), w_reduce, chip, r_rows, r_half)
    parts += expand_copies(((ea_own, ea_other, lasts[0]), (eb_own, eb_other, lasts[1])), w_expand, chip, e_rows, e_half)

    @pl.when(step == 0)
    def _():
        handles, first = [], 0
        for part in parts:
            handles += start_all(part, sems, first)
            first += len(part)
        acc_grad[...] = jnp.zeros_like(acc_grad)
        acc_branch[...] = jnp.zeros_like(acc_branch)
        for handle in handles:
            handle.wait()

    at = pl.ds(pl.multiple_of(step * chunk, chunk), chunk)
    n_rows = s_own.shape[0]
    block_r = w_reduce[at, :]
    block_e = w_expand[:, at]
    sums = jnp.zeros((1, chunk), F32)
    for side, scaled in enumerate((s_own, s_other)):
        rows = slice(side * n_rows, (side + 1) * n_rows)
        grad_pre = dot_tb(scaled[...], block_r) * slope[rows, :]
        sums += col_sum(grad_pre)
        rounded = grad_pre.astype(BF)
        grad_pre_ref[rows, :] = rounded
        acc_grad[rows, :] += dot_tb(rounded, block_e)
        acc_branch[rows, :] += dot(act[rows, :], block_r)
    bias_ref[...] = sums

    @pl.when(step == pl.num_programs(0) - 1)
    def _():
        grad_own_ref[...] = acc_grad[:n_rows, :]
        grad_send_ref[...] = acc_grad[n_rows:, :].astype(BF)
        branch_own_ref[...] = acc_branch[:n_rows, :]
        branch_send_ref[...] = acc_branch[n_rows:, :].astype(BF)


def reduce(ids, s_own, s_other, act, slope, expand_w, reduce_w, lasts, e_rows, r_rows, chunk):
    n_rows, width = s_own.shape
    hidden = act.shape[-1]
    n_sems = 8 * expand_w[0].shape[0]
    by_col = pl.BlockSpec((2 * n_rows, chunk), lambda i, *_: (0, i))
    row = whole((n_rows, width))
    layout = (e_rows, hidden // 2, r_rows, width // 2, lasts, chunk)
    return call(
        functools.partial(reduce_kernel, layout),
        "reduce",
        [
            jax.ShapeDtypeStruct((2 * n_rows, hidden), BF),
            jax.ShapeDtypeStruct((1, hidden), F32),
            jax.ShapeDtypeStruct((n_rows, width), F32),
            jax.ShapeDtypeStruct((n_rows, width), BF),
            jax.ShapeDtypeStruct((n_rows, width), F32),
            jax.ShapeDtypeStruct((n_rows, width), BF),
        ],
        (s_own, s_other, act, slope, *expand_w, *reduce_w),
        [row, row, by_col, by_col] + [ANY] * 8,
        [by_col, pl.BlockSpec((1, chunk), lambda i, *_: (0, i)), row, row, row, row],
        grid=(hidden // chunk,),
        scalars=(ids,),
        scratch=[
            pltpu.VMEM((width, hidden), BF),
            pltpu.VMEM((hidden, width), BF),
            pltpu.VMEM((2 * n_rows, width), F32),
            pltpu.VMEM((2 * n_rows, width), F32),
            pltpu.SemaphoreType.DMA((n_sems,)),
        ],
        flops=12 * n_rows * width * hidden,
        limit=56,
    )


def chip_grad_kernel(layout, ids, left_own, left_other, right_own, right_other, keep_a, send_a, keep_b, send_b):
    block, half, firsts, n_chips, split_right = layout
    chip = ids[0]
    if right_other is None:
        right = right_own[...]
    else:
        right = jnp.concatenate([right_own[...], right_other[...]], axis=0)
    for rel in range(n_chips):
        at = chip ^ rel
        cols = pl.ds(pl.multiple_of(at * block, block), block)
        if left_other is None:
            left = left_own[:, cols]
        else:
            left = jnp.concatenate([left_own[:, cols], left_other[:, cols]], axis=0)
        product = dot_ta(left, right)
        for keep, send, first, part in ((keep_a, send_a, firsts[0], 0), (keep_b, send_b, firsts[1], 1)):
            slot = remove_bit(at, first)
            value = product[:, part * half : (part + 1) * half]
            if bit_at(rel, first):
                send[slot] = value.astype(BF)
            else:
                keep[slot] = value


def chip_grad(name, ids, left, right, n_chips, firsts):
    left = left if len(left) == 2 else (left[0], None)
    right = right if len(right) == 2 else (right[0], None)
    block = left[0].shape[1] // n_chips
    half = right[0].shape[1] // 2
    shape = (n_chips // 2, block, half)
    arrays = [a for a in (*left, *right) if a is not None]
    present = [a is not None for a in (*left, *right)]
    layout = (block, half, firsts, n_chips, None)

    def kernel(ids_ref, *refs):
        given = iter(refs[: len(arrays)])
        ins = [next(given) if there else None for there in present]
        chip_grad_kernel(layout, ids_ref, *ins, *refs[len(arrays) :])

    rows = sum(a.shape[0] for a in left if a is not None)
    return call(
        kernel,
        name,
        [jax.ShapeDtypeStruct(shape, F32), jax.ShapeDtypeStruct(shape, BF)] * 2,
        arrays,
        [whole(a.shape) for a in arrays],
        [whole(shape)] * 4,
        scalars=(ids,),
        flops=2 * rows * left[0].shape[1] * right[0].shape[1],
    )


def core_grad_kernel(layout, ids, *refs):
    n_terms, n_chips, rows, extra = layout
    lefts, rights = refs[:n_terms], refs[n_terms : 2 * n_terms]
    refs = refs[2 * n_terms :]
    vector = None
    if extra:
        vector, refs = refs[0], refs[1:]
    keep, send = refs
    core = ids[1]
    width = rights[0].shape[-1]
    for chip in range(n_chips):
        cols = slice(chip * 2 * rows, (chip + 1) * 2 * rows)
        total = None
        for left, right in zip(lefts, rights, strict=True):
            for image in range(left.shape[0]):
                term = dot_ta(left[image, :, cols], right[image])
                total = term if total is None else total + term
        if extra:
            block = vector[:, cols]
            filled = jnp.concatenate([block, jnp.zeros((LANES - block.shape[0], 2 * rows), F32)], axis=0)
            total = jnp.concatenate([total, filled.T], axis=1)
        first, second = total[:rows], total[rows:]
        keep[chip] = jnp.where(core == 0, first, second)
        send[chip] = jnp.where(core == 0, second, first).astype(BF)


def core_grad(name, ids, lefts, rights, n_chips, vector=None):
    width = rights[0].shape[-1]
    rows = lefts[0].shape[-1] // (2 * n_chips)
    extra = vector is not None
    shape = (n_chips, rows, width + (LANES if extra else 0))
    args = [*lefts, *rights] + ([vector] if extra else [])
    count = sum(a.shape[0] * a.shape[1] for a in lefts)
    return call(
        functools.partial(core_grad_kernel, (len(lefts), n_chips, rows, extra)),
        name,
        [jax.ShapeDtypeStruct(shape, F32), jax.ShapeDtypeStruct(shape, BF)],
        args,
        [whole(a.shape) for a in args],
        [whole(shape)] * 2,
        scalars=(ids,),
        flops=2 * count * lefts[0].shape[-1] * width,
    )


def norm_two_kernel(layout, ids, counts, own, got, middle_ref, branch_ref, cot, params, w_own, w_other, *refs):
    n_images, block_len, group, n_blocks, chunks = layout
    grad_ref, scaled_ref, vec_ref = refs[:3]
    outs, (weight, sems) = refs[3:-2], refs[-2:]
    core, z = ids[1], ids[2]
    handles = start_all(core_copies(w_own, w_other, weight, core), sems)
    slot = lax.broadcasted_iota(jnp.int32, (block_len, 1), 0)
    grads = []
    for image in range(n_images):
        valid = jnp.where(slot < counts[image], 1.0, 0.0)
        grads.append(cot[image * block_len : (image + 1) * block_len, :].astype(F32) * valid)
    grad_y = jnp.concatenate(grads, axis=0)
    normed, inv_std = normalize(middle_ref[...])
    grad_hidden = own[...] + got[...].astype(F32)
    grad_middle = grad_y + norm_back(grad_hidden, normed, inv_std, params[6:7, :])
    grad_ref[...] = grad_middle
    scaled = params[5:6, :] * grad_middle
    rounded = scaled.astype(BF)
    scaled_ref[...] = rounded
    vec_ref[0:1, :] = col_sum(scaled)
    vec_ref[1:2, :] = col_sum(grad_middle * branch_ref[...])
    vec_ref[2:3, :] = col_sum(grad_hidden * normed)
    vec_ref[3:4, :] = col_sum(grad_hidden)
    vec_ref[4:8, :] = jnp.zeros((4, vec_ref.shape[1]), F32)
    for handle in handles:
        handle.wait()
    n = 0
    for rel in n_blocks:
        rows = pl.ds(pl.multiple_of((z ^ rel) * group, group), group)
        grad_att = dot_tb(rounded, weight[rows, :]).astype(BF)
        for first, count in chunks:
            outs[n][...] = grad_att[first * block_len : (first + count) * block_len].reshape(count, block_len, group)
            n += 1


def norm_two(ids, counts, own, got, middle, branch, cot, params, w_own, w_other, n_images, group, order, chunks):
    rows, width = own.shape
    block_len = rows // n_images
    outs = [
        jax.ShapeDtypeStruct((rows, width), F32),
        jax.ShapeDtypeStruct((rows, width), BF),
        jax.ShapeDtypeStruct((8, width), F32),
    ]
    outs += [jax.ShapeDtypeStruct((count, block_len, group), BF) for _ in order for _, count in chunks]
    full = whole((rows, width))
    return call(
        functools.partial(norm_two_kernel, (n_images, block_len, group, order, chunks)),
        "norm_two",
        outs,
        (own, got, middle, branch, cot, params, w_own, w_other),
        [full] * 5 + [whole(params.shape), ANY, ANY],
        [whole(o.shape) for o in outs],
        scalars=(ids, counts),
        scratch=[pltpu.VMEM((width, width), BF), pltpu.SemaphoreType.DMA((2 * w_own.shape[0],))],
        flops=2 * rows * width * width,
    )


def output_kernel(layout, counts, own, got, middle, cot, params, out_ref, vec_ref):
    n_images, block_len = layout
    slot = lax.broadcasted_iota(jnp.int32, (block_len, 1), 0)
    sums = [jnp.zeros((1, params.shape[1]), F32)] * 2
    for image in range(n_images):
        rows = slice(image * block_len, (image + 1) * block_len)
        valid = jnp.where(slot < counts[image], 1.0, 0.0)
        branch = own[rows, :] + got[rows, :].astype(F32) + params[8:9, :]
        grad_y = cot[rows, :].astype(F32) * valid
        out_ref[rows, :] = (valid * (middle[rows, :] + params[9:10, :] * branch)).astype(BF)
        sums[0] = sums[0] + col_sum(params[9:10, :] * grad_y)
        sums[1] = sums[1] + col_sum(grad_y * branch)
    vec_ref[0:1, :] = sums[0]
    vec_ref[1:2, :] = sums[1]
    vec_ref[2:8, :] = jnp.zeros((6, params.shape[1]), F32)


def output_of(counts, own, got, middle, cot, params, n_images):
    rows, width = own.shape
    full = whole((rows, width))
    return call(
        functools.partial(output_kernel, (n_images, rows // n_images)),
        "output",
        [jax.ShapeDtypeStruct((rows, width), BF), jax.ShapeDtypeStruct((8, width), F32)],
        (own, got, middle, cot, params),
        [full] * 4 + [whole(params.shape)],
        [full, whole((8, width))],
        scalars=(counts,),
        flops=10 * rows * width,
    )


def attend_back_kernel(sizes, ids, counts, *refs):
    n_pieces, n_blocks, block_len, width, group = sizes
    pieces, refs = refs[:n_pieces], refs[n_pieces:]
    att_refs, refs = refs[:n_blocks], refs[n_blocks:]
    grad_refs, refs = refs[:n_blocks], refs[n_blocks:]
    mixed_ref, total_ref, params, w_own, w_other, refs = refs[0], refs[1], refs[2], refs[3], refs[4], refs[5:]
    grad_mixed_ref, keep_ref, send_ref, vec_ref, pair_ref, weight, sems = refs
    core = ids[1]
    image = pl.program_id(0)

    @pl.when(image == 0)
    def _():
        vec_ref[...] = jnp.zeros_like(vec_ref)
        pair_ref[...] = jnp.zeros_like(pair_ref)
        for handle in start_all(core_copies(w_own, w_other, weight, core), sems):
            handle.wait()

    valid = key_mask(counts, image, n_blocks, block_len)
    low, masks = head_halves()
    attended = stacked_rows(att_refs)
    grad_att = stacked_rows(grad_refs)
    totals = total_ref[0]
    for pair in range(group // PAIR):
        cols = slice(pair * PAIR, (pair + 1) * PAIR)
        queries = mixed_ref[0, :, cols]
        keys = mixed_ref[0, :, group + pair * PAIR : group + (pair + 1) * PAIR]
        values = mixed_ref[0, :, 2 * group + pair * PAIR : 2 * group + (pair + 1) * PAIR]
        grad = grad_att[:, cols]
        weighted = grad.astype(F32) * attended[:, cols].astype(F32)
        parts = []
        for side in range(2):
            at = 2 * pair + side
            scores = dot_tb(queries * masks[side], keys) * SCALE
            probs = jnp.where(valid, jnp.exp(scores - totals[:, at : at + 1]), 0.0)
            delta = jnp.sum(jnp.where(low if side == 0 else ~low, weighted, 0.0), axis=-1, keepdims=True)
            grad_prob = dot_tb(grad * masks[side], values)
            grad_scores = (probs * (grad_prob - delta) * SCALE).astype(BF)
            parts.append(
                (dot(grad_scores, keys), dot_ta(grad_scores, queries), dot_ta(probs.astype(BF), grad))
            )
        merged = [jnp.where(low, parts[0][n], parts[1][n]) for n in range(3)]
        for n in range(3):
            grad_mixed_ref[0, :, n * group + pair * PAIR : n * group + (pair + 1) * PAIR] = merged[n].astype(BF)
        pair_ref[0:1, cols] += col_sum(merged[0])
        pair_ref[1:2, cols] += col_sum(merged[2])
    inputs = stacked_rows(pieces).astype(F32)
    normed, _ = normalize(inputs)
    grad_hidden = dot_tb(grad_mixed_ref[0], weight[:, : 3 * group])
    vec_ref[0:1, :] += col_sum(grad_hidden * normed)
    vec_ref[1:2, :] += col_sum(grad_hidden)
    half = n_blocks // 2
    for block in range(n_blocks):
        rows = grad_hidden[block * block_len : (block + 1) * block_len]
        if block < half:
            keep_ref[block, 0] = rows
        else:
            send_ref[block - half, 0] = rows.astype(BF)


def attend_back(ids, counts, pieces, att, grad_att, mixed, totals, params, w_own, w_other, n_blocks, group):
    n_images, block_len, width = pieces[0].shape
    slots = n_blocks * block_len
    half = n_blocks // 2
    sizes = (len(pieces), n_blocks, block_len, width, group)
    outs = [
        jax.ShapeDtypeStruct((n_images, slots, 3 * group), BF),
        jax.ShapeDtypeStruct((half, n_images, block_len, width), F32),
        jax.ShapeDtypeStruct((half, n_images, block_len, width), BF),
        jax.ShapeDtypeStruct((8, width), F32),
        jax.ShapeDtypeStruct((8, group), F32),
    ]
    blocks = pl.BlockSpec((half, 1, block_len, width), lambda i, *_: (0, i, 0, 0))
    return call(
        functools.partial(attend_back_kernel, sizes),
        "attend_back",
        outs,
        (*pieces, *att, *grad_att, mixed, totals, params, w_own, w_other),
        piece_specs(pieces, block_len, width)
        + [per_image((block_len, group))] * (2 * n_blocks)
        + [per_image((slots, 3 * group)), per_image((slots, LANES)), whole(params.shape), ANY, ANY],
        [per_image((slots, 3 * group)), blocks, blocks, whole((8, width)), whole((8, group))],
        grid=(n_images,),
        scalars=(ids, counts),
        scratch=[pltpu.VMEM((width, w_own.shape[-1]), BF), pltpu.SemaphoreType.DMA((2 * w_own.shape[0],))],
        flops=n_images * 2 * slots * group * (3 * width + 10 * slots),
    )


def gather_chips(piece, chip, order):
    have = []
    current = piece
    for n, at in enumerate(order):
        got = swap(current, "dp", 2 << at)
        if n == len(order) - 1:
            shape = (-1,) + piece.shape
            return current.reshape(shape), got.reshape(shape)
        have = sorted(have + [at], reverse=True)
        current = join(current, got, bit_at(chip, at) == 1, have.index(at))


def scatter_chips(keep, send, chip, order):
    have = sorted(order[1:], reverse=True)
    lead = (2,) * len(have)
    for n, at in enumerate(order):
        got = swap(send, "dp", 2 << at)
        if n == len(order) - 1:
            return keep, got
        base = keep.shape[1:]
        keep, got = keep.reshape(lead + base), got.reshape(lead + base)
        axis = have.index(order[n + 1])
        mine = bit_at(chip, order[n + 1])

        def side(index):
            pick = lambda a: lax.dynamic_index_in_dim(a, index, axis, keepdims=False)
            return pick(keep) + pick(got).astype(F32)

        send, keep = side(1 - mine).astype(BF), side(mine)
        have.remove(order[n + 1])
        lead = (2,) * len(have)
        shape = (-1,) + base
        send, keep = send.reshape(shape), keep.reshape(shape)


def gather_ctx(piece, z):
    current = piece[None]
    distance = lax.axis_size("ctx") // 2
    while distance:
        got = swap(current, "ctx", distance)
        current = join(current, got, (z & distance) != 0, 1)
        current = current.reshape((-1,) + piece.shape)
        distance //= 2
    return current


def scatter_ctx(value, z):
    distance = 1
    while distance < lax.axis_size("ctx"):
        pairs = value.reshape((-1, 2) + value.shape[1:])
        mine = (z & distance) // distance
        pick = lambda index: lax.dynamic_index_in_dim(pairs, index, 1, keepdims=False)
        got = swap(pick(1 - mine).astype(BF), "ctx", distance)
        value = pick(mine) + got.astype(F32)
        distance *= 2
    return value[0]


def shards(tokens, block_counts, qkv_weight, proj_weight, expand_weight, reduce_weight, vectors, expand_bias, cotangent):
    n_images, block_len, width = tokens.shape
    n_ctx, n_dp = lax.axis_size("ctx"), lax.axis_size("dp")
    n_chips = n_dp // 2
    rows = n_images * block_len
    shard = qkv_weight.shape[0]
    hidden = expand_weight.shape[1]
    half_hidden = hidden // 2
    group = width // n_ctx
    per_row = hidden // width
    z = lax.axis_index("ctx")
    place = lax.axis_index("dp")
    chip, core = place >> 1, place & 1
    ids = jnp.stack([chip, core, z]).astype(jnp.int32)
    up = list(range(bits_of(n_chips)))
    down = up[::-1]
    chunks = ((0, 1), (1, n_images - 1)) if n_images > 1 else ((0, 1),)

    order = [0]
    distance = n_ctx // 2
    while distance:
        order += [rel ^ distance for rel in order]
        distance //= 2

    def gather_tokens(first, count):
        pieces = [tokens[first : first + count]]
        step = n_ctx // 2
        while step:
            send = pieces[0] if len(pieces) == 1 else jnp.concatenate(
                [p.reshape((-1,) + pieces[0].shape) for p in pieces], axis=0
            )
            pieces.append(swap(send, "ctx", step))
            step //= 2
        return pieces

    small = jnp.concatenate([vectors.T, expand_bias.reshape(per_row, shard).T], axis=1)
    small = jnp.pad(small, ((0, 0), (0, LANES - small.shape[1])))
    by_group = qkv_weight.reshape(shard, 3, n_ctx, group).transpose(2, 0, 1, 3).reshape(n_ctx, shard, 3 * group)
    packed = jnp.concatenate([by_group, jnp.broadcast_to(small[None], (n_ctx, shard, LANES))], axis=-1)
    packed = lax.all_to_all(packed, "ctx", split_axis=0, concat_axis=0, tiled=True)
    packed = packed.reshape(n_ctx * shard, 3 * group + LANES)
    parts = gather_chips(packed, chip, up)
    qkv_own = join(parts[0], parts[1], bit_at(chip, up[-1]) == 1, 0).reshape((n_chips,) + packed.shape)
    qkv_other = swap(qkv_own, "dp", 1)

    token_pieces = [gather_tokens(*chunk) for chunk in chunks]

    first_pack = gather_ctx(jnp.concatenate([expand_weight, proj_weight], axis=1), z)
    first_pack = first_pack.reshape(n_ctx * shard, hidden + width)
    by_core = first_pack[:, :hidden].reshape(n_ctx * shard, n_chips, 2, n_ctx * expand_bias.shape[0])
    mine = jnp.where(core == 1, by_core[:, :, 1], by_core[:, :, 0]).reshape(n_ctx * shard, half_hidden)
    theirs = jnp.where(core == 1, by_core[:, :, 0], by_core[:, :, 1]).reshape(n_ctx * shard, half_hidden)
    expand_rows = join(mine, swap(theirs, "dp", 1), core == 1, 0).reshape(2 * n_ctx * shard, half_hidden)
    pack_a = jnp.concatenate([expand_rows[:, : half_hidden // 2], first_pack[:, hidden:]], axis=0)
    pack_b = expand_rows[:, half_hidden // 2 :]
    expand_a = gather_chips(pack_a, chip, up)
    expand_b = gather_chips(pack_b, chip, down)
    expand_w = (*expand_a, *expand_b)
    e_rows = 2 * n_ctx * shard
    proj_own = join(
        expand_a[0][:, e_rows:].reshape((-1, e_rows // 2, width)),
        expand_a[1][:, e_rows:].reshape((-1, e_rows // 2, width)),
        bit_at(chip, up[-1]) == 1,
        0,
    ).reshape(n_chips, e_rows // 2, width)
    proj_other = swap(proj_own, "dp", 1)
    reduce_rows = gather_ctx(reduce_weight, z).reshape(-1, width)
    r_rows = reduce_rows.shape[0]
    reduce_a = gather_chips(reduce_rows[:, : width // 2], chip, up)
    reduce_b = gather_chips(reduce_rows[:, width // 2 :], chip, down)
    reduce_w = (*reduce_a, *reduce_b)
    gather_lasts = (up[-1], down[-1])

    counts_rel = jnp.stack([lax.dynamic_index_in_dim(block_counts, z ^ rel, 1, keepdims=False) for rel in order], axis=1)
    own_counts = counts_rel[:, 0]
    forward = []
    for (first, count), pieces in zip(chunks, token_pieces, strict=True):
        forward.append(attend(ids, counts_rel[first : first + count], pieces, qkv_own, qkv_other, n_ctx, group))
    params = forward[0][0]

    cot = cotangent.reshape(rows, width)
    own_tokens = tokens.reshape(rows, width)
    row_valid = (jnp.arange(block_len, dtype=jnp.int32)[None, :] < own_counts[:, None]).astype(F32).reshape(rows, 1)
    scaled_two = (params[9:10] * (cot.astype(F32) * row_valid)).astype(BF)
    scaled_other = swap(scaled_two, "dp", 1)

    att, chunk_rows = [], []
    for (first, count), outs in zip(chunks, forward, strict=True):
        for block, rel in enumerate(order):
            piece = outs[4 + block].reshape(count * block_len, group)
            att.append(piece if rel == 0 else swap(piece, "ctx", rel))
            chunk_rows.append((rel, first * block_len, count * block_len))
    attended, branch_one, middle, hidden_two = project(
        ids, att, tuple(chunk_rows), group, own_tokens, proj_own, proj_other, params
    )

    hidden_other = swap(hidden_two, "dp", 1)
    bias_all = params[10 : 10 + per_row].reshape(per_row, n_chips, 2, n_ctx, shard)
    bias_row = jnp.where(core == 1, bias_all[:, :, 1], bias_all[:, :, 0]).transpose(1, 2, 0, 3).reshape(1, half_hidden)
    chunk_cols = min(512, half_hidden // 2)
    act, slope = expand(ids, hidden_two, hidden_other, bias_row, expand_w, gather_lasts, e_rows, chunk_cols)
    scatter_firsts = (up[0], down[0])
    reduce_grads = chip_grad("reduce_grad", ids, (act,), (scaled_two, scaled_other), n_chips, scatter_firsts)
    grad_pre, bias_sum, grad_own, grad_send, branch_own, branch_send = reduce(
        ids, scaled_two, scaled_other, act, slope, expand_w, reduce_w, gather_lasts, e_rows, r_rows, chunk_cols
    )
    grad_got = swap(grad_send, "dp", 1)
    expand_grads = chip_grad("expand_grad", ids, (hidden_two, hidden_other), (grad_pre,), n_chips, scatter_firsts)
    outs = norm_two(
        ids, own_counts, grad_own, grad_got, middle, branch_one, cot, params, proj_own, proj_other,
        n_images, group, tuple(order), chunks,
    )
    grad_middle, scaled_one, vec_two = outs[:3]
    branch_got = swap(branch_send, "dp", 1)
    output, vec_out = output_of(own_counts, branch_own, branch_got, middle, cot, params, n_images)

    grads = outs[3:]
    backward = []
    for n, ((first, count), pieces, fwd) in enumerate(zip(chunks, token_pieces, forward, strict=True)):
        grad_att = []
        for block, rel in enumerate(order):
            piece = grads[block * len(chunks) + n]
            grad_att.append(piece if rel == 0 else swap(piece, "ctx", rel))
        backward.append(
            attend_back(
                ids, counts_rel[first : first + count], pieces, fwd[4:], grad_att, fwd[2], fwd[3], params,
                qkv_own, qkv_other, n_ctx, group,
            )
        )
    proj_keep, proj_send = core_grad("proj_grad", ids, [attended[None]], [scaled_one[None]], n_chips)

    vec_one = sum(b[3] for b in backward)
    pair_sums = sum(b[4] for b in backward)
    placed = lax.dynamic_update_slice(jnp.zeros((2, width), F32), pair_sums[:2], (0, z * group))
    bias_lanes = bias_sum.reshape(n_chips, n_ctx, per_row, shard).transpose(2, 0, 1, 3)
    bias_lanes = jnp.where(
        (jnp.arange(2) == core)[None, None, :, None, None], bias_lanes[:, :, None], 0.0
    ).reshape(per_row, width)
    sums = jnp.concatenate([vec_one[:2], placed, vec_two[:4], vec_out[:2], bias_lanes], axis=0)
    sums = jnp.pad(sums, ((0, 16 - sums.shape[0]), (0, 0)))
    qkv_keep, qkv_send = core_grad(
        "qkv_grad", ids, [f[1] for f in forward], [b[0] for b in backward], n_chips, sums
    )

    def after_core(keep, send):
        got = swap(send, "dp", 1)
        total = keep + got.astype(F32)
        lead = total.reshape((2,) * len(up) + total.shape[1:])
        axis = len(up) - 1 - up[0]
        pick = lambda index: lax.dynamic_index_in_dim(lead, index, axis, keepdims=False).reshape((-1,) + total.shape[1:])
        mine = bit_at(chip, up[0])
        last, got = scatter_chips(pick(mine), pick(1 - mine).astype(BF), chip, up)
        return (last + got.astype(F32)).reshape((n_ctx, shard) + total.shape[2:])

    def scattered(parts, base):
        sides = []
        for keep, send, route in ((parts[0], parts[1], up), (parts[2], parts[3], down)):
            last, got = scatter_chips(keep, send, chip, route)
            sides.append((last + got.astype(F32)).reshape(base))
        return jnp.concatenate(sides, axis=-1)

    reduce_sum = scattered(reduce_grads, (n_ctx, reduce_weight.shape[0], width // 2))
    reduce_out = scatter_ctx(reduce_sum, z)

    expand_sum = scattered(expand_grads, (2, n_ctx, shard, half_hidden // 2))
    expand_mine = scatter_ctx(expand_sum.transpose(1, 0, 2, 3), z)
    expand_keep = lax.dynamic_index_in_dim(expand_mine, core, 0, keepdims=False)
    expand_got = swap(lax.dynamic_index_in_dim(expand_mine, 1 - core, 0, keepdims=False).astype(BF), "dp", 1)
    cols = (shard, n_chips, half_hidden // n_chips)
    expand_out = join(expand_keep.reshape(cols), expand_got.astype(F32).reshape(cols), core == 1, 2)
    expand_out = expand_out.reshape(shard, hidden)

    proj_out = scatter_ctx(after_core(proj_keep, proj_send), z)

    qkv_all = lax.all_to_all(
        after_core(qkv_keep, qkv_send).astype(BF), "ctx", split_axis=0, concat_axis=0, tiled=True
    ).astype(F32)
    qkv_out = qkv_all[:, :, : 3 * group].reshape(n_ctx, shard, 3, group).transpose(1, 2, 0, 3).reshape(shard, 3 * width)
    vec_all = jnp.sum(qkv_all[:, :, 3 * group :], axis=0).T
    n_vec = vectors.shape[0]
    vec_grad = vec_all[:n_vec]
    bias_grad = vec_all[n_vec : n_vec + per_row].reshape(-1)

    input_parts = []
    for (first, count), back in zip(chunks, backward, strict=True):
        keep, send = back[1], back[2]
        distance = 1
        while True:
            got = swap(send, "ctx", distance)
            total = keep + got.astype(F32)
            distance *= 2
            if distance >= n_ctx:
                break
            half = total.shape[0] // 2
            keep, send = total[:half], total[half:].astype(BF)
        part = slice(first, first + count)
        normed, inv_std = normalize(tokens[part].astype(F32))
        grads_in = grad_middle.reshape(n_images, block_len, width)[part]
        input_parts.append((grads_in + norm_back(total[0], normed, inv_std, params[0])).astype(BF))
    input_grad = jnp.concatenate(input_parts, axis=0)

    return (
        output.reshape(n_images, block_len, width),
        input_grad,
        qkv_out,
        proj_out,
        expand_out,
        reduce_out,
        vec_grad,
        bias_grad,
    )


def solution(mesh):
    row = P(("dp", "ctx"), None)
    act = P("dp", "ctx", None)
    return jax.shard_map(
        shards,
        mesh=mesh,
        in_specs=(act, P("dp", None), row, row, row, row, P(None, ("dp", "ctx")), P(("dp", "ctx")), act),
        out_specs=(act, act, row, row, row, row, P(None, ("dp", "ctx")), P(("dp", "ctx"))),
        check_vma=False,
    )
```
